32 devices in a mesh: seq: 4 (over y, x), tp: 8 (over z, core).
Axes of the slice: x: 2, y: 2, z: 4, core: 2. Of those that a mesh axis runs over, the one named last changes fastest.
Arguments:
- tokens: bfloat16 [2048, 2560], P('seq'), may hold values from -6 to 6
- expert_ids: int32 [2048, 6], P('seq'), may hold values from 0 to 15, all different within a row; in each aligned block of 512 rows (0 to 511, 512 to 1023, ...) at most 288 rows name the same one
- gate_weights: bfloat16 [2048, 6], P('seq'), may hold values from 0.049804688 to 0.34960938
- live: int32 [2048], P('seq'), may hold values 0 or 1
- norm_gain: float32 [2560], replicated, may hold values from 0.5 to 1.5
- expert_gate: bfloat16 [16, 1536, 2560], P('tp', 'seq'), may hold values from -0.125 to 0.125
- expert_up: bfloat16 [16, 1536, 2560], P('tp', 'seq'), may hold values from -0.125 to 0.125
- expert_down: bfloat16 [16, 1536, 2560], P('tp', 'seq'), may hold values from -0.15625 to 0.15625
- shared_gate: bfloat16 [1536, 2560], P('seq'), may hold values from -0.125 to 0.125
- shared_up: bfloat16 [1536, 2560], P('seq'), may hold values from -0.125 to 0.125
- shared_down: bfloat16 [1536, 2560], P('seq'), may hold values from -0.15625 to 0.15625
Outputs:
- mixed: bfloat16 [2048, 2560], P(('seq', 'tp'))
The draws below stay inside these ranges and needn't reach their ends.
Inputs may be any that keep to these rules, and one draw needn't show every extreme that they name: `expert_ids`: each row names 6 different experts. In each aligned block of 512 rows (the tokens of one index of seq) no expert is named by more than 288 rows, a bound that some block reaches.
All inputs are finite; a program needn't handle non-finite values. No bound on the sum of `live` on one device may be relied on, other than what follows from the above.
Results may differ from the reference program's by a relative error of at most 0.017.
Values may be sent and summed in bfloat16 or wider, within the bound.
A program may use at most 128 MiB of HBM per device.

```python
import math
import jax
import jax.numpy as jnp
import numpy as np
from jax import lax

D = 2560
FF = 1536
TOP = 6
SH = 1536
TOK_SEQ = 512
EXPERTS = 16
TOKENS = 2048
CAP = 288
N_SEQ = 4


def place_ends(entries, stream_key, least, top_value):
    longest = entries.shape.index(max(entries.shape))
    spots = []
    for shift in (0, 1):
        where = [jax.random.randint(jax.random.fold_in(stream_key, axis), (), 0, length) for axis, length in enumerate(entries.shape)]
        where[longest] = (where[longest] + shift) % entries.shape[longest]
        spots.append(tuple(where))
    return entries.at[spots[0]].set(least).at[spots[1]].set(top_value)


def block_scale(rng, dims, split, smallest, top_value):
    loudness, own = 1.0, jax.random.fold_in(rng, 6)
    for axis_at, parts in split:
        heights = jnp.exp(jax.random.uniform(jax.random.fold_in(own, axis_at), (parts,), jnp.float32, smallest / len(split), top_value / len(split)))
        loudness = loudness * jnp.repeat(heights, dims[axis_at] // parts).reshape([-1 if axis == axis_at else 1 for axis in range(len(dims))])
    return loudness


def deal_out(own_key, own, number, rows, count, top, reach, skew):
    sequence = jax.random.permutation(own_key, count)
    crowded, ordinary = shares(count, rows * top, reach, skew, True), shares(count, rows * top, reach, skew, False)
    places = jnp.arange(count)

    def named(sizes, turn):
        used = int((sizes > 0).sum())
        fixed = max(1, used // 4)
        moved = fixed + (places - fixed + turn * (used - fixed)) % max(1, count - fixed)
        return jnp.zeros((count,), jnp.int32).at[sequence[jnp.where(places < fixed, places, moved)]].set(jnp.asarray(sizes, jnp.int32))

    sizes = jnp.where(number % 4 == 0, named(crowded, number // 4), named(ordinary, number - number // 4 - 1))
    mixed = jax.random.permutation(jax.random.fold_in(own, 3), count)
    donor, receiver = mixed[0:count // 2 * 2:2], mixed[1:count // 2 * 2:2]
    margin = jnp.minimum(sizes[donor] - 1, reach - sizes[receiver]) // 2
    margin = jnp.where((donor == sequence[0]) | (receiver == sequence[0]) | (sizes[receiver] == 0), 0, jnp.maximum(margin, 0))
    moved = jax.random.randint(jax.random.fold_in(own, 4), (count // 2,), 0, 1 << 20) % (margin + 1)
    sizes = sizes.at[donor].add(-moved).at[receiver].add(moved)
    members = jnp.searchsorted(jnp.cumsum(sizes), jnp.arange(rows * top), side="right").astype(jnp.int32)
    listing = members.reshape(top, rows).T
    listing = listing[jax.random.permutation(jax.random.fold_in(own, 1), rows)]
    turn = jax.random.randint(jax.random.fold_in(own, 2), (rows, 1), 0, top)
    return jnp.take_along_axis(listing, (jnp.arange(top)[None, :] + turn) % top, axis=1)


def shares(count, total, bound, lean, full):
    loads = [(1 << 20) // math.isqrt(standing ** lean) + 1 for standing in range(1, count + 1)]
    largest = bound if full else min(bound, max(-(-total // count), total * loads[0] // sum(loads)))
    least = 1 if total - largest >= count - 1 else 0
    given, rest = [largest] + [least] * (count - 1), total - largest - least * (count - 1)
    while rest > 0:
        free = [i for i in range(1, count) if given[i] < largest] or [i for i in range(1, count) if given[i] < bound]
        mass, remaining = sum([loads[i] for i in free]), rest
        for i in free:
            extra = min(bound - given[i], max(1, remaining * loads[i] // mass), rest)
            given[i] = given[i] + extra
            rest = rest - extra
    return np.array(given)


def bell_draw(stream_key, dims, spread, reach, pieces=(), kind=jnp.bfloat16):
    loudness = block_scale(stream_key, dims, pieces, -0.22, 0.18) if pieces else 1.0
    array = jax.random.normal(stream_key, dims, jnp.float32) * spread * loudness
    return jnp.minimum(jnp.maximum(array, -reach), reach).astype(kind)


def setup_inputs(seed: int = 0) -> dict:
    streams_of = jax.random.split(jax.random.key(seed), 12)
    tokens = bell_draw(streams_of[0], (TOKENS, D), 1.0, 6.0, ((0, 4),))
    expert_ids_keys = jax.random.split(jax.random.fold_in(streams_of[1], 1), TOKENS // TOK_SEQ)
    expert_ids_turns = jax.random.permutation(jax.random.fold_in(streams_of[1], 3), TOKENS // TOK_SEQ)
    expert_ids = jax.vmap(lambda own, number: deal_out(jax.random.fold_in(streams_of[1], 2), own, number, TOK_SEQ, EXPERTS, TOP, CAP, 2))(expert_ids_keys, expert_ids_turns).reshape((TOKENS, TOP))
    gate_weights = jnp.clip(0.049804688 + 0.2998047 * jax.random.uniform(streams_of[2], (TOKENS, TOP), jnp.float32) ** block_scale(streams_of[2], (TOKENS, TOP), ((0, 4),), -0.2, 0.2), 0.049804688, 0.34960938).astype(jnp.bfloat16)
    live = place_ends((jax.random.randint(streams_of[3], (TOKENS,), 0, 8) < 7).astype(jnp.int32), jax.random.fold_in(streams_of[3], 1), 0, 1)
    norm_gain = jnp.clip(1.0 + 0.1 * jax.random.normal(streams_of[4], (D,), jnp.float32), 0.5, 1.5)
    expert_gate = bell_draw(streams_of[5], (EXPERTS, FF, D), D ** -0.5, 0.125, ((0, 8), (1, 4)))
    expert_up = bell_draw(streams_of[6], (EXPERTS, FF, D), D ** -0.5, 0.125, ((0, 8), (1, 4)))
    expert_down = bell_draw(streams_of[7], (EXPERTS, FF, D), FF ** -0.5, 0.15625, ((0, 8), (1, 4)))
    shared_gate = bell_draw(streams_of[8], (SH, D), D ** -0.5, 0.125, ((0, 4),))
    shared_up = bell_draw(streams_of[9], (SH, D), D ** -0.5, 0.125, ((0, 4),))
    shared_down = bell_draw(streams_of[10], (SH, D), SH ** -0.5, 0.15625, ((0, 4),))
    return {"tokens": tokens, "expert_ids": expert_ids, "gate_weights": gate_weights, "live": live, "norm_gain": norm_gain, "expert_gate": expert_gate, "expert_up": expert_up, "expert_down": expert_down, "shared_gate": shared_gate, "shared_up": shared_up, "shared_down": shared_down}


def ffn_blocks(rows, w_gate, w_up, w_down, blocks):
    gate_part = jnp.einsum('rd,hd->rh', rows, w_gate, preferred_element_type=jnp.float32)
    up_part = jnp.einsum('rd,hd->rh', rows, w_up, preferred_element_type=jnp.float32)
    hidden = (jax.nn.silu(gate_part) * up_part).astype(jnp.bfloat16)
    row_count = rows.shape[0]
    inner = w_down.shape[0] // blocks
    split_hidden = hidden.astype(jnp.float32).reshape(row_count, blocks, inner)
    split_down = w_down.astype(jnp.float32).reshape(blocks, inner, w_down.shape[1])
    partial_sums = jnp.einsum('rjh,jhd->rjd', split_hidden, split_down)
    rounded = lax.optimization_barrier(partial_sums.astype(jnp.bfloat16))
    return lax.optimization_barrier(jnp.sum(rounded.astype(jnp.float32), axis=1))

def reference(tokens, expert_ids, gate_weights, live, norm_gain, expert_gate, expert_up, expert_down, shared_gate, shared_up, shared_down):
    values = tokens.astype(jnp.float32)
    scale = lax.rsqrt(lax.optimization_barrier(jnp.mean(values * values, axis=-1, keepdims=True)) + 1e-05)
    normed = (values * scale * norm_gain).astype(jnp.bfloat16)
    weight_eff = gate_weights.astype(jnp.float32) * live.astype(jnp.float32)[:, None]
    ids_blocks = expert_ids.reshape(N_SEQ, TOK_SEQ, TOP)
    weight_blocks = weight_eff.reshape(N_SEQ, TOK_SEQ, TOP)
    block_index = jnp.broadcast_to(jnp.arange(N_SEQ, dtype=jnp.int32)[:, None], (N_SEQ, TOK_SEQ)).astype(jnp.int32)
    token_index = (block_index * TOK_SEQ + jnp.arange(TOK_SEQ, dtype=jnp.int32)[None, :]).astype(jnp.int32)

    def one_expert(routed, inputs):
        w_gate, w_up, w_down, expert_index = inputs
        matches = ids_blocks == expert_index
        matched = jnp.any(matches, axis=-1)
        weight = lax.optimization_barrier(jnp.sum(jnp.where(matches, weight_blocks, jnp.zeros_like(weight_blocks)), axis=-1))
        position = jnp.cumsum(matched.astype(jnp.int32), axis=1).astype(jnp.int32) - 1
        slot_pos = jnp.where(matched, position, CAP).astype(jnp.int32)
        slot_token = jnp.full((N_SEQ, CAP), TOKENS, jnp.int32).at[block_index, slot_pos].set(token_index, mode='drop')
        slot_weight = jnp.zeros((N_SEQ, CAP), jnp.float32).at[block_index, slot_pos].set(weight, mode='drop')
        flat_token = slot_token.reshape(-1).astype(jnp.int32)
        valid = flat_token < TOKENS
        picked = normed[jnp.minimum(flat_token, TOKENS - 1)]
        rows = jnp.where(valid[:, None], picked, jnp.zeros_like(picked))
        expert_out = ffn_blocks(rows, w_gate, w_up, w_down, N_SEQ)
        routed = routed.at[flat_token].add(expert_out * slot_weight.reshape(-1)[:, None], mode='drop')
        return (routed, None)
    routed, unused = lax.scan(one_expert, jnp.zeros((TOKENS, D), jnp.float32), (expert_gate, expert_up, expert_down, jnp.arange(EXPERTS, dtype=jnp.int32)))
    shared_blocks = normed.reshape(N_SEQ, TOK_SEQ, D)
    shared_out = lax.map(lambda rows: ffn_blocks(rows, shared_gate, shared_up, shared_down, N_SEQ), shared_blocks)
    return (routed + shared_out.reshape(TOKENS, D)).astype(jnp.bfloat16)
```

```python
from functools import partial

import jax
import jax.numpy as jnp
from jax import lax
from jax.experimental import pallas as pl
from jax.experimental.pallas import tpu as pltpu
from jax.sharding import PartitionSpec as P

MESH = pl.DeviceIdType.MESH
LANES = 128


def rms_rows(tokens, norm_gain):
    values = tokens.astype(jnp.float32)
    scale = lax.rsqrt(jnp.mean(values * values, axis=-1, keepdims=True) + 1e-05)
    return (values * scale * norm_gain).astype(jnp.bfloat16)


def dot_nt(a, b):
    return lax.dot_general(a, b, (((1,), (1,)), ((), ())), preferred_element_type=jnp.float32)


def silu(v):
    return v / (1.0 + jnp.exp(-v))


def layer_kernel(
    chunks,
    n_z,
    columns,
    width,
    rows_z,
    own_hbm,
    gate_hbm,
    up_hbm,
    down_hbm,
    sgate_hbm,
    sup_hbm,
    sdown_hbm,
    out_ref,
    x_buf,
    part,
    from_sib,
    ring_in,
    z_in,
    gate_w,
    up_w,
    down_w,
    sgate_w,
    sup_w,
    sdown_w,
    hid,
    shid,
    w_sem,
    own_sem,
    send_own,
    send_fwd,
    send_part,
    send_ring,
    send_z,
    recv_x,
    recv_part,
    recv_ring,
    recv_z,
):
    seq = lax.axis_index("seq")
    tp = lax.axis_index("tp")
    core = tp % 2
    zed = tp // 2
    other = 1 - core
    sx = seq % 2
    sy = seq // 2
    nbr_x = sy * 2 + (1 - sx)
    nbr_y = (1 - sy) * 2 + sx
    blk_a = nbr_y * other + nbr_x * core
    blk_b = nbr_x * other + nbr_y * core
    blk_d = 3 - seq
    sib = (seq, zed * 2 + other)
    dev_a = (blk_a, tp)
    dev_b = (blk_b, tp)
    rows = n_z * rows_z
    inner = gate_w.shape[1]

    def remote(src, dst, ssem, rsem, dev):
        return pltpu.make_async_remote_copy(
            src_ref=src, dst_ref=dst, send_sem=ssem, recv_sem=rsem, device_id=dev, device_id_type=MESH
        )

    def own_copy(k, slot, dev):
        return remote(
            own_hbm.at[k], x_buf.at[seq, k, core], send_own.at[k, slot], recv_x.at[k, seq, core], dev
        )

    def x_copy(k, blk, half, slot, dev):
        return remote(
            x_buf.at[blk, k, half],
            x_buf.at[blk, k, half],
            send_fwd.at[k, slot],
            recv_x.at[k, blk, half],
            dev,
        )

    def part_copy(k, blk):
        return remote(
            part.at[blk, k, other],
            from_sib.at[blk, k],
            send_part.at[k, blk],
            recv_part.at[k, blk],
            sib,
        )

    def ring_copy(k, blk, slot, dev):
        return remote(
            part.at[blk, k, core],
            ring_in.at[k, slot],
            send_ring.at[k, slot],
            recv_ring.at[k, slot],
            dev,
        )

    def z_copy(k, src_z, dst_z):
        return remote(
            part.at[seq, k, core, pl.ds(dst_z * rows_z, rows_z)],
            z_in.at[k, src_z],
            send_z.at[k, dst_z],
            recv_z.at[k, src_z],
            (seq, dst_z * 2 + core),
        )

    weight_copies = [
        pltpu.make_async_copy(src, dst, w_sem.at[i])
        for i, (src, dst) in enumerate(
            (
                (gate_hbm, gate_w),
                (up_hbm, up_w),
                (down_hbm, down_w),
                (sgate_hbm, sgate_w),
                (sup_hbm, sup_w),
                (sdown_hbm, sdown_w),
            )
        )
    ]

    def local_own(k):
        return pltpu.make_async_copy(own_hbm.at[k], x_buf.at[seq, k, core], own_sem.at[k])

    barrier = pltpu.get_barrier_semaphore()
    for dev in (sib, dev_a, dev_b):
        pl.semaphore_signal(barrier, inc=1, device_id=dev, device_id_type=MESH)
    for step in range(1, n_z):
        target = (zed + step) % n_z
        pl.semaphore_signal(
            barrier, inc=1, device_id=(seq, target * 2 + core), device_id_type=MESH
        )
    for k in range(chunks):
        local_own(k).start()
    pl.semaphore_wait(barrier, 3 + n_z - 1)

    for k in range(chunks):
        if k < 2:
            own_copy(k, 1, dev_a).start()
            own_copy(k, 2, dev_b).start()
        own_copy(k, 0, sib).start()
    for copy in weight_copies:
        copy.start()
    for k in range(chunks):
        local_own(k).wait()
    for copy in weight_copies:
        copy.wait()

    def unit(k, blk):
        x_all = x_buf[blk, k].reshape(2 * rows, x_buf.shape[-1])
        x = x_all[:, :width]
        listed = x_all[:, width:].astype(jnp.float32)
        lane = lax.broadcasted_iota(jnp.int32, listed.shape, 1)
        for i in range(columns):
            mine = jnp.where(lane == tp * columns + i, listed, 0.0)
            weight = jnp.sum(mine, axis=1, keepdims=True)
            g = dot_nt(x, gate_w[i])
            u = dot_nt(x, up_w[i])
            hid[:, i * inner : (i + 1) * inner] = (silu(g) * u * weight).astype(jnp.bfloat16)
        tile = 512

        @pl.loop(0, width // tile)
        def _(n):
            cols = pl.ds(pl.multiple_of(n * tile, tile), tile)
            p = jnp.dot(hid[...], down_w[:, cols], preferred_element_type=jnp.float32)
            part[blk, k, :, :, cols] = p.astype(jnp.bfloat16).reshape(2, rows, tile)

        part_copy(k, blk).start()

    def shared(k):
        mine = pl.ds(pl.multiple_of(zed * rows_z, rows_z), rows_z)
        x = jnp.concatenate([x_buf[b, k, core, mine, :width] for b in range(4)], axis=0)
        shid[...] = (silu(dot_nt(x, sgate_w[...])) * dot_nt(x, sup_w[...])).astype(jnp.bfloat16)
        tile = 512

        @pl.loop(0, width // tile)
        def _(n):
            cols = pl.ds(pl.multiple_of(n * tile, tile), tile)
            p = jnp.dot(shid[...], sdown_w[:, cols], preferred_element_type=jnp.float32)
            for b in range(4):
                old = part[b, k, core, mine, cols].astype(jnp.float32)
                new = old + p[b * rows_z : (b + 1) * rows_z]
                part[b, k, core, mine, cols] = new.astype(jnp.bfloat16)

    def add_pair(k, blk):
        part_copy(k, blk).wait_recv()
        total = part[blk, k, core].astype(jnp.float32) + from_sib[blk, k].astype(jnp.float32)
        part[blk, k, core] = total.astype(jnp.bfloat16)

    def ring_one(k):
        add_pair(k, blk_d)
        ring_copy(k, blk_d, 0, dev_a).start()
        add_pair(k, blk_a)
        ring_copy(k, blk_a, 1, dev_a).start()
        add_pair(k, blk_b)
        add_pair(k, seq)

    def ring_two(k):
        ring_copy(k, blk_d, 0, dev_a).wait_recv()
        total = part[blk_b, k, core].astype(jnp.float32) + ring_in[k, 0].astype(jnp.float32)
        part[blk_b, k, core] = total.astype(jnp.bfloat16)
        ring_copy(k, blk_b, 2, dev_b).start()

    def ring_three(k):
        ring_copy(k, blk_a, 1, dev_a).wait_recv()
        ring_copy(k, blk_b, 2, dev_b).wait_recv()
        total = (
            part[seq, k, core].astype(jnp.float32)
            + ring_in[k, 1].astype(jnp.float32)
            + ring_in[k, 2].astype(jnp.float32)
        )
        part[seq, k, core] = total.astype(jnp.bfloat16)
        for step in range(1, n_z):
            z_copy(k, zed, (zed + step) % n_z).start()

    def finish(k):
        total = part[
            seq, k, core, pl.ds(pl.multiple_of(zed * rows_z, rows_z), rows_z)
        ].astype(jnp.float32)
        for step in range(1, n_z):
            source = (zed + step) % n_z
            z_copy(k, source, source).wait_recv()
            total = total + z_in[k, source].astype(jnp.float32)
        out_ref[k] = total.astype(jnp.bfloat16)

    @pl.loop(0, chunks)
    def _(k):
        own_copy_in = x_copy(k, seq, other, 0, sib)
        own_copy_in.wait_recv()
        unit(k, seq)
        x_copy(k, blk_b, core, 0, sib).wait_recv()
        x_copy(k, blk_b, core, 3, dev_a).start()
        x_copy(k, blk_b, core, 1, sib).start()
        x_copy(k, blk_a, core, 0, sib).wait_recv()
        x_copy(k, blk_a, core, 0, sib).start()

        @pl.when(k + 2 < chunks)
        def _():
            own_copy(k + 2, 1, dev_a).start()
            own_copy(k + 2, 2, dev_b).start()

        @pl.when(k > 0)
        def _():
            ring_two(k - 1)

        x_copy(k, blk_b, other, 0, sib).wait_recv()
        unit(k, blk_b)
        x_copy(k, blk_a, other, 0, sib).wait_recv()
        unit(k, blk_a)
        x_copy(k, blk_d, core, 0, sib).wait_recv()
        x_copy(k, blk_d, core, 2, sib).start()

        @pl.when(k > 0)
        def _():
            ring_three(k - 1)

        x_copy(k, blk_d, other, 0, sib).wait_recv()
        unit(k, blk_d)
        shared(k)
        ring_one(k)

    ring_two(chunks - 1)
    ring_three(chunks - 1)

    @pl.loop(0, chunks)
    def _(k):
        finish(k)
        own_copy(k, 0, sib).wait_send()
        own_copy(k, 1, dev_a).wait_send()
        own_copy(k, 2, dev_b).wait_send()
        x_copy(k, blk_a, core, 0, sib).wait_send()
        x_copy(k, blk_b, core, 1, sib).wait_send()
        x_copy(k, blk_d, core, 2, sib).wait_send()
        x_copy(k, blk_b, core, 3, dev_a).wait_send()
        for b in range(4):
            part_copy(k, b).wait_send()
        ring_copy(k, blk_d, 0, dev_a).wait_send()
        ring_copy(k, blk_a, 1, dev_a).wait_send()
        ring_copy(k, blk_b, 2, dev_b).wait_send()
        for step in range(1, n_z):
            z_copy(k, zed, (zed + step) % n_z).wait_send()


def on_device(
    tokens,
    expert_ids,
    gate_weights,
    live,
    norm_gain,
    expert_gate,
    expert_up,
    expert_down,
    shared_gate,
    shared_up,
    shared_down,
):
    tok_seq, width = tokens.shape
    columns, inner = expert_gate.shape[:2]
    s_inner = shared_gate.shape[0]
    n_seq = lax.axis_size("seq")
    n_tp = lax.axis_size("tp")
    assert n_seq == 4
    tok_dev = tok_seq // n_tp
    n_z = n_tp // 2
    chunks = max(1, min(2, tok_dev // 16))
    rows_z = tok_dev // chunks
    rows = n_z * rows_z
    experts = columns * n_tp
    pad = -(-experts // LANES) * LANES
    core = lax.axis_index("tp") % 2

    def half(a):
        split = a.reshape((n_z, 2, chunks, rows_z) + a.shape[1:])
        picked = lax.dynamic_index_in_dim(split, core, 1, keepdims=False)
        return jnp.swapaxes(picked, 0, 1).reshape((chunks * rows,) + a.shape[1:])

    normed = rms_rows(half(tokens), norm_gain)
    ids = half(expert_ids)
    weights = half(gate_weights).astype(jnp.float32) * half(live).astype(jnp.float32)[:, None]
    matches = ids[:, :, None] == jnp.arange(pad, dtype=jnp.int32)[None, None, :]
    listed = jnp.sum(jnp.where(matches, weights[:, :, None], 0.0), axis=1).astype(jnp.bfloat16)
    own = jnp.concatenate([normed, listed], axis=1).reshape(chunks, rows, width + pad)

    bf16 = jnp.bfloat16
    dma = pltpu.SemaphoreType.DMA
    out = pl.pallas_call(
        partial(layer_kernel, chunks, n_z, columns, width, rows_z),
        out_shape=jax.ShapeDtypeStruct((chunks, rows_z, width), bf16),
        in_specs=[pl.BlockSpec(memory_space=pl.ANY)] * 7,
        out_specs=pl.BlockSpec(memory_space=pltpu.VMEM),
        scratch_shapes=[
            pltpu.VMEM((4, chunks, 2, rows, width + pad), bf16),
            pltpu.VMEM((4, chunks, 2, rows, width), bf16),
            pltpu.VMEM((4, chunks, rows, width), bf16),
            pltpu.VMEM((chunks, 3, rows, width), bf16),
            pltpu.VMEM((chunks, n_z, rows_z, width), bf16),
            pltpu.VMEM((columns, inner, width), bf16),
            pltpu.VMEM((columns, inner, width), bf16),
            pltpu.VMEM((columns * inner, width), bf16),
            pltpu.VMEM((s_inner, width), bf16),
            pltpu.VMEM((s_inner, width), bf16),
            pltpu.VMEM((s_inner, width), bf16),
            pltpu.VMEM((2 * rows, columns * inner), bf16),
            pltpu.VMEM((4 * rows_z, s_inner), bf16),
            dma((6,)),
            dma((chunks,)),
            dma((chunks, 3)),
            dma((chunks, 4)),
            dma((chunks, 4)),
            dma((chunks, 3)),
            dma((chunks, n_z)),
            dma((chunks, 4, 2)),
            dma((chunks, 4)),
            dma((chunks, 3)),
            dma((chunks, n_z)),
        ],
        compiler_params=pltpu.CompilerParams(
            collective_id=0, has_side_effects=True, vmem_limit_bytes=62 * 1024 * 1024
        ),
    )(
        own,
        expert_gate,
        expert_up,
        expert_down.reshape(columns * inner, width),
        shared_gate,
        shared_up,
        shared_down,
    )
    return out.reshape(tok_dev, width)


def solution(mesh):
    placed = (
        P("seq", None),
        P("seq", None),
        P("seq", None),
        P("seq"),
        P(),
        P("tp", "seq", None),
        P("tp", "seq", None),
        P("tp", "seq", None),
        P("seq", None),
        P("seq", None),
        P("seq", None),
    )
    return jax.shard_map(
        on_device, mesh=mesh, in_specs=placed, out_specs=P(("seq", "tp"), None), check_vma=False
    )
```

```python
from functools import partial

import jax
import jax.numpy as jnp
from jax import lax
from jax.experimental import pallas as pl
from jax.experimental.pallas import tpu as pltpu
from jax.sharding import PartitionSpec as P

MESH = pl.DeviceIdType.MESH
LANES = 128


def dot_nt(a, b):
    return lax.dot_general(a, b, (((1,), (1,)), ((), ())), preferred_element_type=jnp.float32)


def silu(v):
    return v / (1.0 + jnp.exp(-v))


def layer_kernel(
    chunks,
    n_z,
    columns,
    width,
    rows_z,
    share,
    ahead,
    tok_hbm,
    gain_ref,
    listed_ref,
    gate_hbm,
    up_hbm,
    down_hbm,
    sgate_hbm,
    sup_hbm,
    sdown_hbm,
    out_ref,
    x_buf,
    part,
    from_sib,
    ring_in,
    z_in,
    gate_w,
    up_w,
    down_w,
    sgate_w,
    sup_w,
    sdown_w,
    hid,
    shid,
    tok_v,
    w_sem,
    own_sem,
    send_own,
    send_fwd,
    send_part,
    send_ring,
    send_z,
    recv_x,
    recv_part,
    recv_ring,
    recv_z,
):
    seq = lax.axis_index("seq")
    tp = lax.axis_index("tp")
    core = tp % 2
    zed = tp // 2
    other = 1 - core
    sx = seq % 2
    sy = seq // 2
    nbr_x = sy * 2 + (1 - sx)
    nbr_y = (1 - sy) * 2 + sx
    blk_a = nbr_y * other + nbr_x * core
    blk_b = nbr_x * other + nbr_y * core
    blk_d = 3 - seq
    sib = (seq, zed * 2 + other)
    dev_a = (blk_a, tp)
    dev_b = (blk_b, tp)
    rows = n_z * rows_z
    parity = zed % 2
    dev_z = (seq, (zed + 1 - 2 * parity) * 2 + core)
    fetched = pl.ds(pl.multiple_of(parity * share, 16), rows - share)
    passed = pl.ds(pl.multiple_of(parity * (rows - share), 16), share)
    given = pl.ds(pl.multiple_of((1 - parity) * (rows - share), 16), share)
    inner = gate_w.shape[1]

    def remote(src, dst, ssem, rsem, dev):
        return pltpu.make_async_remote_copy(
            src_ref=src, dst_ref=dst, send_sem=ssem, recv_sem=rsem, device_id=dev, device_id_type=MESH
        )

    def own_copy(k, slot, dev):
        return x_copy(k, seq, core, fetched, send_own.at[k, slot], 0, dev)

    def own_sib(k, half):
        return x_copy(k, seq, half, pl.ds(0, rows), send_own.at[k, 0], 2, sib)

    def x_copy(k, blk, half, span, ssem, kind, dev):
        ref = x_buf.at[blk, k, half, span]
        return remote(ref, ref, ssem, recv_x.at[k, blk, kind], dev)

    def net(k, blk):
        return x_copy(k, blk, core, fetched, send_fwd.at[k, 0], 0, dev_a)

    def relay(k):
        return x_copy(k, blk_b, core, fetched, send_fwd.at[k, 0], 0, dev_a)

    def over_z(k, blk, slot):
        return x_copy(k, blk, core, passed, send_fwd.at[k, slot], 1, dev_z)

    def from_z(k, blk):
        return x_copy(k, blk, core, given, send_fwd.at[k, 0], 1, dev_z)

    def sib_net(k, blk, half, slot):
        return x_copy(k, blk, half, fetched, send_fwd.at[k, slot], 2, sib)

    def sib_z(k, blk, half, slot):
        return x_copy(k, blk, half, given, send_fwd.at[k, slot], 3, sib)

    def got_net(k, blk, slot):
        net(k, blk).wait_recv()
        over_z(k, blk, slot).start()
        sib_net(k, blk, core, slot + 3).start()

    def got_z(k, blk, slot):
        from_z(k, blk).wait_recv()
        sib_z(k, blk, core, slot + 6).start()

    def got_sib(k, blk):
        sib_net(k, blk, other, 0).wait_recv()
        sib_z(k, blk, other, 0).wait_recv()

    def part_copy(k, blk):
        return remote(
            part.at[blk, k, other],
            from_sib.at[blk, k],
            send_part.at[k, blk],
            recv_part.at[k, blk],
            sib,
        )

    def ring_copy(k, blk, slot, dev):
        return remote(
            part.at[blk, k, core],
            ring_in.at[k, slot],
            send_ring.at[k, slot],
            recv_ring.at[k, slot],
            dev,
        )

    def z_copy(k, src_z, dst_z):
        return remote(
            part.at[seq, k, core, pl.ds(dst_z * rows_z, rows_z)],
            z_in.at[k, src_z],
            send_z.at[k, dst_z],
            recv_z.at[k, src_z],
            (seq, dst_z * 2 + core),
        )

    weight_copies = [
        pltpu.make_async_copy(src, dst, w_sem.at[i])
        for i, (src, dst) in enumerate(
            (
                (gate_hbm, gate_w),
                (up_hbm, up_w),
                (down_hbm, down_w),
                (sgate_hbm, sgate_w),
                (sup_hbm, sup_w),
                (sdown_hbm, sdown_w),
            )
        )
    ]

    def load_own(k):
        return pltpu.make_async_copy(tok_hbm.at[:, core, k], tok_v.at[k], own_sem.at[k])

    def norm_own(k):
        values = tok_v[k].reshape(rows, width).astype(jnp.float32)
        scale = lax.rsqrt(jnp.mean(values * values, axis=-1, keepdims=True) + 1e-05)
        x_buf[seq, k, core, :, :width] = (values * scale * gain_ref[...]).astype(jnp.bfloat16)
        x_buf[seq, k, core, :, width:] = listed_ref[k]

    barrier = pltpu.get_barrier_semaphore()
    for dev in (sib, dev_a, dev_b):
        pl.semaphore_signal(barrier, inc=1, device_id=dev, device_id_type=MESH)
    for step in range(1, n_z):
        target = (zed + step) % n_z
        pl.semaphore_signal(
            barrier, inc=1, device_id=(seq, target * 2 + core), device_id_type=MESH
        )
    for k in range(chunks):
        load_own(k).start()
    for k in range(chunks):
        load_own(k).wait()
        norm_own(k)
        if k == 0:
            pl.semaphore_wait(barrier, 3 + n_z - 1)
        if k < ahead:
            own_copy(k, 1, dev_a).start()
            own_copy(k, 2, dev_b).start()
        own_sib(k, core).start()
    for copy in weight_copies:
        copy.start()
    for copy in weight_copies:
        copy.wait()

    def unit(k, blk):
        x_all = x_buf[blk, k].reshape(2 * rows, x_buf.shape[-1])
        x = x_all[:, :width]
        listed = x_all[:, width:].astype(jnp.float32)
        lane = lax.broadcasted_iota(jnp.int32, listed.shape, 1)
        for i in range(columns):
            mine = jnp.where(lane == tp * columns + i, listed, 0.0)
            weight = jnp.sum(mine, axis=1, keepdims=True)
            g = dot_nt(x, gate_w[i])
            u = dot_nt(x, up_w[i])
            hid[:, i * inner : (i + 1) * inner] = (silu(g) * u * weight).astype(jnp.bfloat16)
        tile = 512

        @pl.loop(0, width // tile)
        def _(n):
            cols = pl.ds(pl.multiple_of(n * tile, tile), tile)
            p = jnp.dot(hid[...], down_w[:, cols], preferred_element_type=jnp.float32)
            part[blk, k, :, :, cols] = p.astype(jnp.bfloat16).reshape(2, rows, tile)

        part_copy(k, blk).start()

    def shared(k):
        mine = pl.ds(pl.multiple_of(zed * rows_z, rows_z), rows_z)
        x = jnp.concatenate([x_buf[b, k, core, mine, :width] for b in range(4)], axis=0)
        shid[...] = (silu(dot_nt(x, sgate_w[...])) * dot_nt(x, sup_w[...])).astype(jnp.bfloat16)
        tile = 512

        @pl.loop(0, width // tile)
        def _(n):
            cols = pl.ds(pl.multiple_of(n * tile, tile), tile)
            p = jnp.dot(shid[...], sdown_w[:, cols], preferred_element_type=jnp.float32)
            for b in range(4):
                old = part[b, k, core, mine, cols].astype(jnp.float32)
                new = old + p[b * rows_z : (b + 1) * rows_z]
                part[b, k, core, mine, cols] = new.astype(jnp.bfloat16)

    def add_pair(k, blk):
        part_copy(k, blk).wait_recv()
        total = part[blk, k, core].astype(jnp.float32) + from_sib[blk, k].astype(jnp.float32)
        part[blk, k, core] = total.astype(jnp.bfloat16)

    def ring_one(k):
        add_pair(k, blk_d)
        ring_copy(k, blk_d, 0, dev_a).start()
        add_pair(k, blk_a)
        ring_copy(k, blk_a, 1, dev_a).start()
        add_pair(k, blk_b)
        add_pair(k, seq)

    def ring_two(k):
        ring_copy(k, blk_d, 0, dev_a).wait_recv()
        total = part[blk_b, k, core].astype(jnp.float32) + ring_in[k, 0].astype(jnp.float32)
        part[blk_b, k, core] = total.astype(jnp.bfloat16)
        ring_copy(k, blk_b, 2, dev_b).start()

    def ring_three(k):
        ring_copy(k, blk_a, 1, dev_a).wait_recv()
        ring_copy(k, blk_b, 2, dev_b).wait_recv()
        total = (
            part[seq, k, core].astype(jnp.float32)
            + ring_in[k, 1].astype(jnp.float32)
            + ring_in[k, 2].astype(jnp.float32)
        )
        part[seq, k, core] = total.astype(jnp.bfloat16)
        for step in range(1, n_z):
            z_copy(k, zed, (zed + step) % n_z).start()

    def finish(k):
        total = part[
            seq, k, core, pl.ds(pl.multiple_of(zed * rows_z, rows_z), rows_z)
        ].astype(jnp.float32)
        for step in range(1, n_z):
            source = (zed + step) % n_z
            z_copy(k, source, source).wait_recv()
            total = total + z_in[k, source].astype(jnp.float32)
        out_ref[k] = total.astype(jnp.bfloat16)

    def service(k):
        net(k, blk_b).wait_recv()
        relay(k).start()
        over_z(k, blk_b, 2).start()
        sib_net(k, blk_b, core, 5).start()
        got_net(k, blk_a, 1)

        @pl.when(k + ahead < chunks)
        def _():
            own_copy(k + ahead, 1, dev_a).start()
            own_copy(k + ahead, 2, dev_b).start()

    @pl.loop(0, chunks)
    def _(k):
        own_sib(k, other).wait_recv()
        unit(k, seq)

        @pl.when(k == 0)
        def _():
            service(k)

        @pl.when(k > 0)
        def _():
            ring_two(k - 1)

        got_z(k, blk_b, 2)
        got_z(k, blk_a, 1)
        got_sib(k, blk_b)
        unit(k, blk_b)
        got_net(k, blk_d, 3)
        got_sib(k, blk_a)
        unit(k, blk_a)

        @pl.when(k > 0)
        def _():
            ring_three(k - 1)

        got_z(k, blk_d, 3)
        got_sib(k, blk_d)

        @pl.when(k + 1 < chunks)
        def _():
            service(k + 1)

        unit(k, blk_d)
        shared(k)
        ring_one(k)

    ring_two(chunks - 1)
    ring_three(chunks - 1)

    @pl.loop(0, chunks)
    def _(k):
        finish(k)
        own_sib(k, core).wait_send()
        own_copy(k, 1, dev_a).wait_send()
        own_copy(k, 2, dev_b).wait_send()
        relay(k).wait_send()
        for slot, blk in ((1, blk_a), (2, blk_b), (3, blk_d)):
            over_z(k, blk, slot).wait_send()
            sib_net(k, blk, core, slot + 3).wait_send()
            sib_z(k, blk, core, slot + 6).wait_send()
        for b in range(4):
            part_copy(k, b).wait_send()
        ring_copy(k, blk_d, 0, dev_a).wait_send()
        ring_copy(k, blk_a, 1, dev_a).wait_send()
        ring_copy(k, blk_b, 2, dev_b).wait_send()
        for step in range(1, n_z):
            z_copy(k, zed, (zed + step) % n_z).wait_send()


def on_device(
    tokens,
    expert_ids,
    gate_weights,
    live,
    norm_gain,
    expert_gate,
    expert_up,
    expert_down,
    shared_gate,
    shared_up,
    shared_down,
):
    tok_seq, width = tokens.shape
    columns, inner = expert_gate.shape[:2]
    s_inner = shared_gate.shape[0]
    n_seq = lax.axis_size("seq")
    n_tp = lax.axis_size("tp")
    assert n_seq == 4
    tok_dev = tok_seq // n_tp
    n_z = n_tp // 2
    chunks = max(1, min(2, tok_dev // 16))
    rows_z = tok_dev // chunks
    rows = n_z * rows_z
    experts = columns * n_tp
    pad = -(-experts // LANES) * LANES
    core = lax.axis_index("tp") % 2

    def half(a):
        split = a.reshape((n_z, 2, chunks, rows_z) + a.shape[1:])
        picked = lax.dynamic_index_in_dim(split, core, 1, keepdims=False)
        return jnp.swapaxes(picked, 0, 1).reshape((chunks * rows,) + a.shape[1:])

    ids = half(expert_ids)
    weights = half(gate_weights).astype(jnp.float32) * half(live).astype(jnp.float32)[:, None]
    matches = ids[:, :, None] == jnp.arange(pad, dtype=jnp.int32)[None, None, :]
    listed = jnp.sum(jnp.where(matches, weights[:, :, None], 0.0), axis=1).astype(jnp.bfloat16)
    listed = listed.reshape(chunks, rows, pad)
    share = rows * 5 // 256 * 16

    bf16 = jnp.bfloat16
    dma = pltpu.SemaphoreType.DMA
    out = pl.pallas_call(
        partial(layer_kernel, chunks, n_z, columns, width, rows_z, share, 1),
        out_shape=jax.ShapeDtypeStruct((chunks, rows_z, width), bf16),
        in_specs=[
            pl.BlockSpec(memory_space=pl.ANY),
            pl.BlockSpec(memory_space=pltpu.VMEM),
            pl.BlockSpec(memory_space=pltpu.VMEM),
        ]
        + [pl.BlockSpec(memory_space=pl.ANY)] * 6,
        out_specs=pl.BlockSpec(memory_space=pltpu.VMEM),
        scratch_shapes=[
            pltpu.VMEM((4, chunks, 2, rows, width + pad), bf16),
            pltpu.VMEM((4, chunks, 2, rows, width), bf16),
            pltpu.VMEM((4, chunks, rows, width), bf16),
            pltpu.VMEM((chunks, 3, rows, width), bf16),
            pltpu.VMEM((chunks, n_z, rows_z, width), bf16),
            pltpu.VMEM((columns, inner, width), bf16),
            pltpu.VMEM((columns, inner, width), bf16),
            pltpu.VMEM((columns * inner, width), bf16),
            pltpu.VMEM((s_inner, width), bf16),
            pltpu.VMEM((s_inner, width), bf16),
            pltpu.VMEM((s_inner, width), bf16),
            pltpu.VMEM((2 * rows, columns * inner), bf16),
            pltpu.VMEM((4 * rows_z, s_inner), bf16),
            pltpu.VMEM((chunks, n_z, rows_z, width), bf16),
            dma((6,)),
            dma((chunks,)),
            dma((chunks, 3)),
            dma((chunks, 10)),
            dma((chunks, 4)),
            dma((chunks, 3)),
            dma((chunks, n_z)),
            dma((chunks, 4, 4)),
            dma((chunks, 4)),
            dma((chunks, 3)),
            dma((chunks, n_z)),
        ],
        compiler_params=pltpu.CompilerParams(
            collective_id=0, has_side_effects=True, vmem_limit_bytes=62 * 1024 * 1024
        ),
    )(
        tokens.reshape(n_z, 2, chunks, rows_z, width),
        norm_gain.reshape(1, width),
        listed,
        expert_gate,
        expert_up,
        expert_down.reshape(columns * inner, width),
        shared_gate,
        shared_up,
        shared_down,
    )
    return out.reshape(tok_dev, width)


def solution(mesh):
    placed = (
        P("seq", None),
        P("seq", None),
        P("seq", None),
        P("seq"),
        P(),
        P("tp", "seq", None),
        P("tp", "seq", None),
        P("tp", "seq", None),
        P("seq", None),
        P("seq", None),
        P("seq", None),
    )
    return jax.shard_map(
        on_device, mesh=mesh, in_specs=placed, out_specs=P(("seq", "tp"), None), check_vma=False
    )
```
